256 devices in a mesh: pipe: 8 (over z_hi, x), dp: 32 (over y, z_lo, core).
Axes of the slice: x: 4, y: 4, z: 8 (z_hi: 2, z_lo: 4; z = z_hi * 4 + z_lo), core: 2. Of those that a mesh axis runs over, the one named last changes fastest.
Arguments:
- samples: bfloat16 [160, 3, 32, 640], P('dp'), may hold values from -6 to 6
- timesteps: int32 [160], P('dp'), may hold values from 0 to 999
- cotangent: bfloat16 [160, 3, 32, 640], P('dp'), may hold values from -0.059814453 to 0.059814453
- spatial_weight: bfloat16 [8, 5760, 640], P('pipe', 'dp'), may hold values from -0.078125 to 0.078125
- temporal_weight: bfloat16 [8, 1920, 640], P('pipe', 'dp'), may hold values from -0.125 to 0.125
Outputs:
- spatial_grad: float32 [8, 5760, 640], P('pipe', 'dp')
- temporal_grad: float32 [8, 1920, 640], P('pipe', 'dp')
The draws below stay inside these ranges and needn't reach their ends.
All inputs are finite; a program needn't handle non-finite values.
Results may differ from the reference program's by a relative error of at most 0.034.
Values may be sent and summed in bfloat16 or wider, within the bound.
A program may use at most 128 MiB of HBM per device.

```python
import math
import jax
import jax.numpy as jnp
from jax import lax

C = 640
FRAMES = 3
HEIGHT = 8
WIDTH = 4
MICRO = 5
STEPS = 1000
PIXELS = 32
SAMPLES = 160
N_PIPE = 8
N_DP = 32


def touch_ends(entries, stream_key, least, largest):
    extent = entries.shape
    place = [jax.random.randint(jax.random.fold_in(stream_key, axis), (), 0, extent[axis]) for axis in range(len(extent))]
    entries = entries.at[tuple(place)].set(least)
    longest = extent.index(max(extent))
    place[longest] = (place[longest] + 1) % extent[longest]
    return entries.at[tuple(place)].set(largest)


def steps_of(own_key, dims, cuts, low, top_value):
    loudness, own = 1.0, jax.random.fold_in(own_key, 6)
    for position, blocks in cuts:
        draws = jnp.exp(jax.random.uniform(jax.random.fold_in(own, position), (blocks,), jnp.float32, low / len(cuts), top_value / len(cuts)))
        loudness = loudness * jnp.repeat(draws, dims[position] // blocks).reshape([-1 if axis == position else 1 for axis in range(len(dims))])
    return loudness


def bell_draw(key, extent, deviation, limit, cuts=(), held_as=jnp.bfloat16):
    factor_of = steps_of(key, extent, cuts, -0.22, 0.18) if cuts else 1.0
    result = jax.random.normal(key, extent, jnp.float32) * deviation * factor_of
    return jnp.minimum(jnp.maximum(result, -limit), limit).astype(held_as)


def setup_inputs(seed: int = 0) -> dict:
    key_of = jax.random.split(jax.random.key(seed), 6)
    return {
        "samples": bell_draw(key_of[0], (SAMPLES, FRAMES, PIXELS, C), 1.0, 6.0, ((0, 32),)),
        "timesteps": touch_ends(jax.random.randint(key_of[1], (SAMPLES,), 0, STEPS), jax.random.fold_in(key_of[1], 1), 0, STEPS - 1).astype(jnp.int32),
        "cotangent": bell_draw(key_of[2], (SAMPLES, FRAMES, PIXELS, C), 0.01, 0.059814453, ((0, 32),)),
        "spatial_weight": bell_draw(key_of[3], (N_PIPE, 9 * C, C), (9 * C) ** -0.5, 0.078125, ((0, 8), (1, 32))),
        "temporal_weight": bell_draw(key_of[4], (N_PIPE, 3 * C, C), (3 * C) ** -0.5, 0.125, ((0, 8), (1, 32))),
    }


def embedding_of(step, channels):
    half_width = channels // 2
    frequency = jnp.exp(-math.log(10000.0) * jnp.arange(half_width, dtype=jnp.float32) / half_width)
    phases = step.astype(jnp.float32) * frequency
    return jnp.concatenate([jnp.sin(phases), jnp.cos(phases)])

def normalize(summed):
    return summed * lax.rsqrt(lax.optimization_barrier(jnp.mean(summed * summed, axis=-1, keepdims=True)) + 1e-06)

def spatial_columns(normed):
    frames, pixels, channels = normed.shape
    grid = normed.reshape(frames, HEIGHT, WIDTH, channels)
    padded = jnp.pad(grid, ((0, 0), (1, 1), (1, 1), (0, 0)))
    pieces = [padded[:, row:row + HEIGHT, col:col + WIDTH, :] for row in range(3) for col in range(3)]
    return jnp.concatenate(pieces, axis=-1).reshape(frames * pixels, 9 * channels)

def spatial_fold(grads, frames, channels):
    parts = grads.reshape(frames, HEIGHT, WIDTH, 9, channels)
    padded = jnp.zeros((frames, HEIGHT + 2, WIDTH + 2, channels), jnp.float32)
    for row in range(3):
        for col in range(3):
            padded = padded.at[:, row:row + HEIGHT, col:col + WIDTH, :].add(parts[:, :, :, row * 3 + col, :])
    return padded[:, 1:HEIGHT + 1, 1:WIDTH + 1, :].reshape(frames, HEIGHT * WIDTH, channels)

def temporal_columns(activated):
    frames, pixels, channels = activated.shape
    padded = jnp.pad(activated, ((1, 1), (0, 0), (0, 0)))
    pieces = [padded[tap:tap + frames] for tap in range(3)]
    return jnp.concatenate(pieces, axis=-1).reshape(frames * pixels, 3 * channels)

def temporal_fold(grads, frames, pixels, channels):
    parts = grads.reshape(frames, pixels, 3, channels)
    padded = jnp.zeros((frames + 2, pixels, channels), jnp.float32)
    for tap in range(3):
        padded = padded.at[tap:tap + frames].add(parts[:, :, tap, :])
    return padded[1:frames + 1]

def section_forward(block_in, embedding, spatial, temporal):
    frames, pixels, channels = block_in.shape
    summed = block_in.astype(jnp.float32) + embedding
    normed = normalize(summed).astype(jnp.bfloat16)
    preact = jnp.dot(spatial_columns(normed), spatial, preferred_element_type=jnp.float32)
    activated = jax.nn.silu(preact).astype(jnp.bfloat16).reshape(frames, pixels, channels)
    mixed = jnp.dot(temporal_columns(activated), temporal, preferred_element_type=jnp.float32)
    return (block_in.astype(jnp.float32) + mixed.reshape(frames, pixels, channels)).astype(jnp.bfloat16)

def section_backward(block_in, embedding, spatial, temporal, upstream):
    frames, pixels, channels = block_in.shape
    summed = block_in.astype(jnp.float32) + embedding
    normed = normalize(summed).astype(jnp.bfloat16)
    columns = spatial_columns(normed)
    preact = jnp.dot(columns, spatial, preferred_element_type=jnp.float32)
    activated = jax.nn.silu(preact).astype(jnp.bfloat16).reshape(frames, pixels, channels)
    tcolumns = temporal_columns(activated)
    upstream_flat = upstream.reshape(frames * pixels, channels)
    temporal_term = jnp.dot(tcolumns.T, upstream_flat, preferred_element_type=jnp.float32)
    act_grad = temporal_fold(jnp.dot(upstream_flat, temporal.T, preferred_element_type=jnp.float32), frames, pixels, channels)
    logistic = jax.nn.sigmoid(preact)
    slope = logistic * (1.0 + preact * (1.0 - logistic))
    pre_grad = (act_grad.reshape(frames * pixels, channels) * slope).astype(jnp.bfloat16)
    spatial_term = jnp.dot(columns.T, pre_grad, preferred_element_type=jnp.float32)
    norm_grad = spatial_fold(jnp.dot(pre_grad, spatial.T, preferred_element_type=jnp.float32), frames, channels)
    _, pullback = jax.vjp(normalize, summed)
    back_input = (upstream.astype(jnp.float32) + pullback(norm_grad)[0]).astype(jnp.bfloat16)
    return (back_input, spatial_term, temporal_term)

def one_sample(sample, step, upstream, spatial_weight, temporal_weight):
    embedding = embedding_of(step, sample.shape[-1])

    def forward(hidden, weights):
        return (section_forward(hidden, embedding, weights[0], weights[1]), hidden)
    _, inputs = lax.scan(forward, sample, (spatial_weight, temporal_weight))

    def backward(carried, pieces):
        back_input, spatial_term, temporal_term = section_backward(pieces[0], embedding, pieces[1], pieces[2], carried)
        return (back_input, (spatial_term, temporal_term))
    _, terms = lax.scan(backward, upstream, (inputs, spatial_weight, temporal_weight), reverse=True)
    return terms

def reference(samples, timesteps, cotangent, spatial_weight, temporal_weight):
    shard_samples = samples.reshape((N_DP, MICRO) + samples.shape[1:])
    shard_steps = timesteps.reshape(N_DP, MICRO)
    shard_cots = cotangent.reshape((N_DP, MICRO) + cotangent.shape[1:])
    zero_sp = jnp.zeros(spatial_weight.shape, jnp.float32)
    zero_tm = jnp.zeros(temporal_weight.shape, jnp.float32)

    def per_shard(totals, shard):

        def per_sample(partial_value, item):
            spatial_term, temporal_term = one_sample(item[0], item[1], item[2], spatial_weight, temporal_weight)
            return ((partial_value[0] + spatial_term, partial_value[1] + temporal_term), None)
        partial_value, _ = lax.scan(per_sample, (zero_sp, zero_tm), shard)
        rounded = lax.optimization_barrier((partial_value[0].astype(jnp.bfloat16), partial_value[1].astype(jnp.bfloat16)))
        return ((totals[0] + rounded[0].astype(jnp.float32), totals[1] + rounded[1].astype(jnp.float32)), None)
    totals, _ = lax.scan(per_shard, (zero_sp, zero_tm), (shard_samples, shard_steps, shard_cots))
    return (totals[0], totals[1])
```

```python
import math

import jax
import jax.numpy as jnp
from jax import lax
from jax.sharding import PartitionSpec as P

HEIGHT = 8
WIDTH = 4


def passed_along(value, axis, steps):
    count = lax.axis_size(axis)
    first, last = (max(0, -steps), min(count, count - steps))
    return lax.ppermute(value, axis, [(source, source + steps) for source in range(first, last)])


def embedding_of(step, channels):
    half_width = channels // 2
    frequency = jnp.exp(-math.log(10000.0) * jnp.arange(half_width, dtype=jnp.float32) / half_width)
    phases = step.astype(jnp.float32) * frequency
    return jnp.concatenate([jnp.sin(phases), jnp.cos(phases)])


def normalize(summed):
    return summed * lax.rsqrt(jnp.mean(summed * summed, axis=-1, keepdims=True) + 1e-06)


def spatial_columns(normed):
    lead = normed.shape[:-2]
    channels = normed.shape[-1]
    grid = normed.reshape(lead + (HEIGHT, WIDTH, channels))
    pad = [(0, 0)] * len(lead) + [(1, 1), (1, 1), (0, 0)]
    padded = jnp.pad(grid, pad)
    pieces = [
        padded[..., row : row + HEIGHT, col : col + WIDTH, :] for row in range(3) for col in range(3)
    ]
    return jnp.concatenate(pieces, axis=-1).reshape(-1, 9 * channels)


def spatial_fold(grads, frames, channels):
    parts = grads.reshape(frames, HEIGHT, WIDTH, 9, channels)
    total = None
    for row in range(3):
        for col in range(3):
            piece = jnp.pad(
                parts[:, :, :, row * 3 + col, :],
                ((0, 0), (row, 2 - row), (col, 2 - col), (0, 0)),
            )
            total = piece if total is None else total + piece
    return total[:, 1 : HEIGHT + 1, 1 : WIDTH + 1, :].reshape(frames, HEIGHT * WIDTH, channels)


def temporal_columns(activated):
    lead = activated.shape[:-3]
    frames = activated.shape[-3]
    channels = activated.shape[-1]
    pad = [(0, 0)] * len(lead) + [(1, 1), (0, 0), (0, 0)]
    padded = jnp.pad(activated, pad)
    pieces = [padded[..., tap : tap + frames, :, :] for tap in range(3)]
    return jnp.concatenate(pieces, axis=-1).reshape(-1, 3 * channels)


def temporal_fold(grads, frames, pixels, channels):
    parts = grads.reshape(frames, pixels, 3, channels)
    total = None
    for tap in range(3):
        piece = jnp.pad(parts[:, :, tap, :], ((tap, 2 - tap), (0, 0), (0, 0)))
        total = piece if total is None else total + piece
    return total[1 : frames + 1]


def section_forward(block_in, embedding, spatial, temporal):
    frames, pixels, channels = block_in.shape
    summed = block_in.astype(jnp.float32) + embedding
    normed = normalize(summed).astype(jnp.bfloat16)
    preact = jnp.dot(spatial_columns(normed), spatial, preferred_element_type=jnp.float32)
    activated = jax.nn.silu(preact).astype(jnp.bfloat16).reshape(frames, pixels, channels)
    mixed = jnp.dot(temporal_columns(activated), temporal, preferred_element_type=jnp.float32)
    out = (block_in.astype(jnp.float32) + mixed.reshape(frames, pixels, channels)).astype(
        jnp.bfloat16
    )
    return out, normed, preact.reshape(frames, pixels, channels), activated


def section_backward(block_in, embedding, spatial, temporal, upstream, preact):
    frames, pixels, channels = block_in.shape
    summed = block_in.astype(jnp.float32) + embedding
    upstream_flat = upstream.reshape(frames * pixels, channels)
    act_grad = temporal_fold(
        jnp.dot(upstream_flat, temporal.T, preferred_element_type=jnp.float32),
        frames,
        pixels,
        channels,
    )
    logistic = jax.nn.sigmoid(preact)
    slope = logistic * (1.0 + preact * (1.0 - logistic))
    pre_grad = (act_grad * slope).astype(jnp.bfloat16)
    norm_grad = spatial_fold(
        jnp.dot(
            pre_grad.reshape(frames * pixels, channels),
            spatial.T,
            preferred_element_type=jnp.float32,
        ),
        frames,
        channels,
    )
    _, pullback = jax.vjp(normalize, summed)
    back_input = (upstream.astype(jnp.float32) + pullback(norm_grad)[0]).astype(jnp.bfloat16)
    return back_input, pre_grad


def per_device(samples, timesteps, cotangent, spatial_weight, temporal_weight):
    sections = lax.axis_size("pipe")
    n_dp = lax.axis_size("dp")
    section_index = lax.axis_index("pipe")
    micro_count = samples.shape[0]
    frames, pixels, channels = (samples.shape[1], samples.shape[2], samples.shape[3])
    moments = jnp.arange(micro_count + sections - 1, dtype=jnp.int32)
    blank = jnp.zeros((frames, pixels, channels), jnp.bfloat16)

    sp_rows = spatial_weight.shape[1]
    tm_rows = temporal_weight.shape[1]
    own_rows = jnp.concatenate([spatial_weight[0], temporal_weight[0]], axis=0)
    gathered = lax.all_gather(own_rows, "dp", axis=0, tiled=False)
    full_spatial = gathered[:, :sp_rows].reshape(n_dp * sp_rows, channels)
    full_temporal = gathered[:, sp_rows:].reshape(n_dp * tm_rows, channels)

    embeddings = jax.vmap(lambda s: embedding_of(s, channels))(timesteps)

    def slot_of(position):
        return jnp.clip(position, -1, micro_count) + 1

    def stash_put(stash, value, slot):
        return lax.dynamic_update_index_in_dim(stash, value, slot, 0)

    def forward_step(carry, moment):
        incoming, s_in, s_normed, s_preact, s_act = carry
        position = moment - section_index
        picked = jnp.clip(position, 0, micro_count - 1)
        slot = slot_of(position)
        own = lax.dynamic_index_in_dim(samples, picked, 0, keepdims=False)
        embedding = lax.dynamic_index_in_dim(embeddings, picked, 0, keepdims=False)
        block_in = jnp.where(section_index == 0, own, incoming)
        result, normed, preact, activated = section_forward(
            block_in, embedding, full_spatial, full_temporal
        )
        s_in = stash_put(s_in, block_in, slot)
        s_normed = stash_put(s_normed, normed.reshape(frames, pixels, channels), slot)
        s_preact = stash_put(s_preact, preact, slot)
        s_act = stash_put(s_act, activated, slot)
        passed = passed_along(result, "pipe", 1)
        return ((passed, s_in, s_normed, s_preact, s_act), None)

    slots = micro_count + 2
    start = (
        blank,
        jnp.zeros((slots, frames, pixels, channels), jnp.bfloat16),
        jnp.zeros((slots, frames, pixels, channels), jnp.bfloat16),
        jnp.zeros((slots, frames, pixels, channels), jnp.float32),
        jnp.zeros((slots, frames, pixels, channels), jnp.bfloat16),
    )
    (_, s_in, s_normed, s_preact, s_act), _ = lax.scan(forward_step, start, moments)

    def backward_step(carry, moment):
        incoming, s_pre, s_up = carry
        position = moment - (sections - 1 - section_index)
        picked = jnp.clip(position, 0, micro_count - 1)
        slot = slot_of(position)
        stored = jnp.clip(position, 0, micro_count - 1) + 1
        block_in = lax.dynamic_index_in_dim(s_in, stored, 0, keepdims=False)
        preact = lax.dynamic_index_in_dim(s_preact, stored, 0, keepdims=False)
        embedding = lax.dynamic_index_in_dim(embeddings, picked, 0, keepdims=False)
        given = lax.dynamic_index_in_dim(cotangent, picked, 0, keepdims=False)
        upstream = jnp.where(section_index == sections - 1, given, incoming)
        back_input, pre_grad = section_backward(
            block_in, embedding, full_spatial, full_temporal, upstream, preact
        )
        s_pre = stash_put(s_pre, pre_grad, slot)
        s_up = stash_put(s_up, upstream, slot)
        passed = passed_along(back_input, "pipe", -1)
        return ((passed, s_pre, s_up), None)

    start = (
        blank,
        jnp.zeros((slots, frames, pixels, channels), jnp.bfloat16),
        jnp.zeros((slots, frames, pixels, channels), jnp.bfloat16),
    )
    (_, s_pre, s_up), _ = lax.scan(backward_step, start, moments)

    normed_all = s_normed[1 : micro_count + 1]
    act_all = s_act[1 : micro_count + 1]
    pre_all = s_pre[1 : micro_count + 1].reshape(-1, channels)
    up_all = s_up[1 : micro_count + 1].reshape(-1, channels)
    spatial_term = lax.dot_general(
        spatial_columns(normed_all), pre_all, (((0,), (0,)), ((), ())),
        preferred_element_type=jnp.float32,
    )
    temporal_term = lax.dot_general(
        temporal_columns(act_all), up_all, (((0,), (0,)), ((), ())),
        preferred_element_type=jnp.float32,
    )
    partial_rows = jnp.concatenate(
        [
            spatial_term.astype(jnp.bfloat16).reshape(n_dp, sp_rows, channels),
            temporal_term.astype(jnp.bfloat16).reshape(n_dp, tm_rows, channels),
        ],
        axis=1,
    )
    share = lax.psum_scatter(partial_rows, "dp", scatter_dimension=0, tiled=False)
    share = share.astype(jnp.float32)
    return (share[None, :sp_rows], share[None, sp_rows:])


def solution(mesh):
    return jax.shard_map(
        per_device,
        mesh=mesh,
        in_specs=(
            P("dp", None, None, None),
            P("dp"),
            P("dp", None, None, None),
            P("pipe", "dp", None),
            P("pipe", "dp", None),
        ),
        out_specs=(P("pipe", "dp", None), P("pipe", "dp", None)),
        check_vma=False,
    )
```

```python
import math

import jax
import jax.numpy as jnp
from jax import lax
from jax.sharding import PartitionSpec as P

HEIGHT = 8
WIDTH = 4


def passed_along(value, axis, steps):
    count = lax.axis_size(axis)
    first, last = (max(0, -steps), min(count, count - steps))
    return lax.ppermute(value, axis, [(source, source + steps) for source in range(first, last)])


def embedding_of(step, channels):
    half_width = channels // 2
    frequency = jnp.exp(-math.log(10000.0) * jnp.arange(half_width, dtype=jnp.float32) / half_width)
    phases = step.astype(jnp.float32) * frequency
    return jnp.concatenate([jnp.sin(phases), jnp.cos(phases)])


def normalize(summed):
    return summed * lax.rsqrt(jnp.mean(summed * summed, axis=-1, keepdims=True) + 1e-06)


def spatial_columns(normed):
    lead = normed.shape[:-2]
    channels = normed.shape[-1]
    grid = normed.reshape(lead + (HEIGHT, WIDTH, channels))
    pad = [(0, 0)] * len(lead) + [(1, 1), (1, 1), (0, 0)]
    padded = jnp.pad(grid, pad)
    pieces = [
        padded[..., row : row + HEIGHT, col : col + WIDTH, :] for row in range(3) for col in range(3)
    ]
    return jnp.concatenate(pieces, axis=-1).reshape(-1, 9 * channels)


def spatial_fold(grads, frames, channels):
    parts = grads.reshape(frames, HEIGHT, WIDTH, 9, channels)
    total = None
    for row in range(3):
        for col in range(3):
            piece = jnp.pad(
                parts[:, :, :, row * 3 + col, :],
                ((0, 0), (row, 2 - row), (col, 2 - col), (0, 0)),
            )
            total = piece if total is None else total + piece
    return total[:, 1 : HEIGHT + 1, 1 : WIDTH + 1, :].reshape(frames, HEIGHT * WIDTH, channels)


def temporal_columns(activated):
    lead = activated.shape[:-3]
    frames = activated.shape[-3]
    channels = activated.shape[-1]
    pad = [(0, 0)] * len(lead) + [(1, 1), (0, 0), (0, 0)]
    padded = jnp.pad(activated, pad)
    pieces = [padded[..., tap : tap + frames, :, :] for tap in range(3)]
    return jnp.concatenate(pieces, axis=-1).reshape(-1, 3 * channels)


def temporal_fold(grads, frames, pixels, channels):
    parts = grads.reshape(frames, pixels, 3, channels)
    total = None
    for tap in range(3):
        piece = jnp.pad(parts[:, :, tap, :], ((tap, 2 - tap), (0, 0), (0, 0)))
        total = piece if total is None else total + piece
    return total[1 : frames + 1]


def section_forward(block_in, embedding, spatial, temporal):
    frames, pixels, channels = block_in.shape
    summed = block_in.astype(jnp.float32) + embedding
    normed = normalize(summed).astype(jnp.bfloat16)
    preact = jnp.dot(spatial_columns(normed), spatial, preferred_element_type=jnp.float32)
    activated = jax.nn.silu(preact).astype(jnp.bfloat16).reshape(frames, pixels, channels)
    mixed = jnp.dot(temporal_columns(activated), temporal, preferred_element_type=jnp.float32)
    out = (block_in.astype(jnp.float32) + mixed.reshape(frames, pixels, channels)).astype(
        jnp.bfloat16
    )
    return out, normed, preact.reshape(frames, pixels, channels), activated


def section_backward(block_in, embedding, spatial, temporal, upstream, preact):
    frames, pixels, channels = block_in.shape
    summed = block_in.astype(jnp.float32) + embedding
    upstream_flat = upstream.reshape(frames * pixels, channels)
    act_grad = temporal_fold(
        jnp.dot(upstream_flat, temporal.T, preferred_element_type=jnp.float32),
        frames,
        pixels,
        channels,
    )
    logistic = jax.nn.sigmoid(preact)
    slope = logistic * (1.0 + preact * (1.0 - logistic))
    pre_grad = (act_grad * slope).astype(jnp.bfloat16)
    norm_grad = spatial_fold(
        jnp.dot(
            pre_grad.reshape(frames * pixels, channels),
            spatial.T,
            preferred_element_type=jnp.float32,
        ),
        frames,
        channels,
    )
    _, pullback = jax.vjp(normalize, summed)
    back_input = (upstream.astype(jnp.float32) + pullback(norm_grad)[0]).astype(jnp.bfloat16)
    return back_input, pre_grad


def per_device(samples, timesteps, cotangent, spatial_weight, temporal_weight):
    sections = lax.axis_size("pipe")
    n_outer = lax.axis_size("dpo")
    n_core = lax.axis_size("core")
    n_dp = n_outer * n_core
    section_index = lax.axis_index("pipe")
    micro_count = samples.shape[0]
    frames, pixels, channels = (samples.shape[1], samples.shape[2], samples.shape[3])
    moments = jnp.arange(micro_count + sections - 1, dtype=jnp.int32)
    blank = jnp.zeros((frames, pixels, channels), jnp.bfloat16)

    sp_rows = spatial_weight.shape[1]
    tm_rows = temporal_weight.shape[1]
    own_rows = jnp.concatenate([spatial_weight[0], temporal_weight[0]], axis=0)
    gathered = lax.all_gather(own_rows, "dpo", axis=0, tiled=False)
    gathered = lax.all_gather(gathered, "core", axis=1, tiled=False)
    gathered = gathered.reshape((n_dp,) + own_rows.shape)
    full_spatial = gathered[:, :sp_rows].reshape(n_dp * sp_rows, channels)
    full_temporal = gathered[:, sp_rows:].reshape(n_dp * tm_rows, channels)

    embeddings = jax.vmap(lambda s: embedding_of(s, channels))(timesteps)

    def slot_of(position):
        return jnp.clip(position, -1, micro_count) + 1

    def stash_put(stash, value, slot):
        return lax.dynamic_update_index_in_dim(stash, value, slot, 0)

    def forward_step(carry, moment):
        incoming, s_in, s_normed, s_preact, s_act = carry
        position = moment - section_index
        picked = jnp.clip(position, 0, micro_count - 1)
        slot = slot_of(position)
        own = lax.dynamic_index_in_dim(samples, picked, 0, keepdims=False)
        embedding = lax.dynamic_index_in_dim(embeddings, picked, 0, keepdims=False)
        block_in = jnp.where(section_index == 0, own, incoming)
        result, normed, preact, activated = section_forward(
            block_in, embedding, full_spatial, full_temporal
        )
        s_in = stash_put(s_in, block_in, slot)
        s_normed = stash_put(s_normed, normed.reshape(frames, pixels, channels), slot)
        s_preact = stash_put(s_preact, preact, slot)
        s_act = stash_put(s_act, activated, slot)
        passed = passed_along(result, "pipe", 1)
        return ((passed, s_in, s_normed, s_preact, s_act), None)

    slots = micro_count + 2
    start = (
        blank,
        jnp.zeros((slots, frames, pixels, channels), jnp.bfloat16),
        jnp.zeros((slots, frames, pixels, channels), jnp.bfloat16),
        jnp.zeros((slots, frames, pixels, channels), jnp.float32),
        jnp.zeros((slots, frames, pixels, channels), jnp.bfloat16),
    )
    (_, s_in, s_normed, s_preact, s_act), _ = lax.scan(forward_step, start, moments)

    def backward_step(carry, moment):
        incoming, s_pre, s_up = carry
        position = moment - (sections - 1 - section_index)
        picked = jnp.clip(position, 0, micro_count - 1)
        slot = slot_of(position)
        stored = jnp.clip(position, 0, micro_count - 1) + 1
        block_in = lax.dynamic_index_in_dim(s_in, stored, 0, keepdims=False)
        preact = lax.dynamic_index_in_dim(s_preact, stored, 0, keepdims=False)
        embedding = lax.dynamic_index_in_dim(embeddings, picked, 0, keepdims=False)
        given = lax.dynamic_index_in_dim(cotangent, picked, 0, keepdims=False)
        upstream = jnp.where(section_index == sections - 1, given, incoming)
        back_input, pre_grad = section_backward(
            block_in, embedding, full_spatial, full_temporal, upstream, preact
        )
        s_pre = stash_put(s_pre, pre_grad, slot)
        s_up = stash_put(s_up, upstream, slot)
        passed = passed_along(back_input, "pipe", -1)
        return ((passed, s_pre, s_up), None)

    start = (
        blank,
        jnp.zeros((slots, frames, pixels, channels), jnp.bfloat16),
        jnp.zeros((slots, frames, pixels, channels), jnp.bfloat16),
    )
    (_, s_pre, s_up), _ = lax.scan(backward_step, start, moments)

    normed_all = s_normed[1 : micro_count + 1]
    act_all = s_act[1 : micro_count + 1]
    pre_all = s_pre[1 : micro_count + 1].reshape(-1, channels)
    up_all = s_up[1 : micro_count + 1].reshape(-1, channels)
    spatial_term = lax.dot_general(
        spatial_columns(normed_all), pre_all, (((0,), (0,)), ((), ())),
        preferred_element_type=jnp.float32,
    )
    temporal_term = lax.dot_general(
        temporal_columns(act_all), up_all, (((0,), (0,)), ((), ())),
        preferred_element_type=jnp.float32,
    )
    partial_rows = jnp.concatenate(
        [
            spatial_term.astype(jnp.bfloat16).reshape(n_dp, sp_rows, channels),
            temporal_term.astype(jnp.bfloat16).reshape(n_dp, tm_rows, channels),
        ],
        axis=1,
    )
    partial_rows = partial_rows.reshape((n_outer, n_core) + partial_rows.shape[1:])
    partial_rows = jnp.swapaxes(partial_rows, 0, 1)
    share = lax.psum_scatter(partial_rows, "core", scatter_dimension=0, tiled=False)
    share = lax.psum_scatter(share, "dpo", scatter_dimension=0, tiled=False)
    share = share.astype(jnp.float32)
    return (share[None, :sp_rows], share[None, sp_rows:])


def solution(mesh):
    n_pipe, n_dp = mesh.devices.shape
    split = jax.sharding.Mesh(mesh.devices.reshape(n_pipe, n_dp // 2, 2), ("pipe", "dpo", "core"))
    dp = ("dpo", "core")
    return jax.shard_map(
        per_device,
        mesh=split,
        in_specs=(
            P(dp, None, None, None),
            P(dp),
            P(dp, None, None, None),
            P("pipe", dp, None),
            P("pipe", dp, None),
        ),
        out_specs=(P("pipe", dp, None), P("pipe", dp, None)),
        check_vma=False,
    )
```

```python
import functools
import math

import jax
import jax.numpy as jnp
from jax import lax
from jax.experimental import pallas as pl
from jax.experimental.pallas import tpu as pltpu
from jax.sharding import PartitionSpec as P

HEIGHT = 8
WIDTH = 4


def hop_kernel(steps, x_ref, out_ref, landing, send_sem, recv_sem):
    count = lax.axis_size("pipe")
    me = lax.axis_index("pipe")
    row = lax.axis_index("dp")
    dest = me + steps
    src = me - steps
    has_dest = (dest >= 0) & (dest < count)
    has_src = (src >= 0) & (src < count)
    barrier = pltpu.get_barrier_semaphore()
    copy = pltpu.make_async_remote_copy(
        src_ref=x_ref,
        dst_ref=landing,
        send_sem=send_sem,
        recv_sem=recv_sem,
        device_id=(dest, row),
        device_id_type=pl.DeviceIdType.MESH,
    )

    @pl.when(has_src)
    def _():
        pl.semaphore_signal(barrier, inc=1, device_id=(src, row), device_id_type=pl.DeviceIdType.MESH)

    @pl.when(has_dest)
    def _():
        pl.semaphore_wait(barrier, 1)
        copy.start()

    @pl.when(has_src)
    def _():
        copy.wait_recv()
        out_ref[...] = landing[...]

    @pl.when(jnp.logical_not(has_src))
    def _():
        out_ref[...] = jnp.zeros_like(out_ref)

    @pl.when(has_dest)
    def _():
        copy.wait_send()


def passed_along(value, axis, steps):
    assert axis == "pipe"
    return pl.pallas_call(
        functools.partial(hop_kernel, steps),
        out_shape=jax.ShapeDtypeStruct(value.shape, value.dtype),
        in_specs=[pl.BlockSpec(memory_space=pltpu.VMEM)],
        out_specs=pl.BlockSpec(memory_space=pltpu.VMEM),
        scratch_shapes=[
            pltpu.VMEM(value.shape, value.dtype),
            pltpu.SemaphoreType.DMA(()),
            pltpu.SemaphoreType.DMA(()),
        ],
        compiler_params=pltpu.CompilerParams(
            collective_id=0 if steps > 0 else 1, has_side_effects=True
        ),
    )(value)


def embedding_of(step, channels):
    half_width = channels // 2
    frequency = jnp.exp(-math.log(10000.0) * jnp.arange(half_width, dtype=jnp.float32) / half_width)
    phases = step.astype(jnp.float32) * frequency
    return jnp.concatenate([jnp.sin(phases), jnp.cos(phases)])


def normalize(summed):
    return summed * lax.rsqrt(jnp.mean(summed * summed, axis=-1, keepdims=True) + 1e-06)


def spatial_columns(normed):
    lead = normed.shape[:-2]
    channels = normed.shape[-1]
    grid = normed.reshape(lead + (HEIGHT, WIDTH, channels))
    pad = [(0, 0)] * len(lead) + [(1, 1), (1, 1), (0, 0)]
    padded = jnp.pad(grid, pad)
    pieces = [
        padded[..., row : row + HEIGHT, col : col + WIDTH, :] for row in range(3) for col in range(3)
    ]
    return jnp.concatenate(pieces, axis=-1).reshape(-1, 9 * channels)


def spatial_fold(grads, frames, channels):
    parts = grads.reshape(frames, HEIGHT, WIDTH, 9, channels)
    total = None
    for row in range(3):
        for col in range(3):
            piece = jnp.pad(
                parts[:, :, :, row * 3 + col, :],
                ((0, 0), (row, 2 - row), (col, 2 - col), (0, 0)),
            )
            total = piece if total is None else total + piece
    return total[:, 1 : HEIGHT + 1, 1 : WIDTH + 1, :].reshape(frames, HEIGHT * WIDTH, channels)


def temporal_columns(activated):
    lead = activated.shape[:-3]
    frames = activated.shape[-3]
    channels = activated.shape[-1]
    pad = [(0, 0)] * len(lead) + [(1, 1), (0, 0), (0, 0)]
    padded = jnp.pad(activated, pad)
    pieces = [padded[..., tap : tap + frames, :, :] for tap in range(3)]
    return jnp.concatenate(pieces, axis=-1).reshape(-1, 3 * channels)


def temporal_fold(grads, frames, pixels, channels):
    parts = grads.reshape(frames, pixels, 3, channels)
    total = None
    for tap in range(3):
        piece = jnp.pad(parts[:, :, tap, :], ((tap, 2 - tap), (0, 0), (0, 0)))
        total = piece if total is None else total + piece
    return total[1 : frames + 1]


def section_forward(block_in, embedding, spatial, temporal):
    frames, pixels, channels = block_in.shape
    summed = block_in.astype(jnp.float32) + embedding
    normed = normalize(summed).astype(jnp.bfloat16)
    preact = jnp.dot(spatial_columns(normed), spatial, preferred_element_type=jnp.float32)
    activated = jax.nn.silu(preact).astype(jnp.bfloat16).reshape(frames, pixels, channels)
    mixed = jnp.dot(temporal_columns(activated), temporal, preferred_element_type=jnp.float32)
    out = (block_in.astype(jnp.float32) + mixed.reshape(frames, pixels, channels)).astype(
        jnp.bfloat16
    )
    return out, normed, preact.reshape(frames, pixels, channels), activated


def section_backward(block_in, embedding, spatial, temporal, upstream, preact):
    frames, pixels, channels = block_in.shape
    summed = block_in.astype(jnp.float32) + embedding
    upstream_flat = upstream.reshape(frames * pixels, channels)
    act_grad = temporal_fold(
        jnp.dot(upstream_flat, temporal.T, preferred_element_type=jnp.float32),
        frames,
        pixels,
        channels,
    )
    logistic = jax.nn.sigmoid(preact)
    slope = logistic * (1.0 + preact * (1.0 - logistic))
    pre_grad = (act_grad * slope).astype(jnp.bfloat16)
    norm_grad = spatial_fold(
        jnp.dot(
            pre_grad.reshape(frames * pixels, channels),
            spatial.T,
            preferred_element_type=jnp.float32,
        ),
        frames,
        channels,
    )
    _, pullback = jax.vjp(normalize, summed)
    back_input = (upstream.astype(jnp.float32) + pullback(norm_grad)[0]).astype(jnp.bfloat16)
    return back_input, pre_grad


def per_device(samples, timesteps, cotangent, spatial_weight, temporal_weight):
    sections = lax.axis_size("pipe")
    n_dp = lax.axis_size("dp")
    section_index = lax.axis_index("pipe")
    micro_count = samples.shape[0]
    frames, pixels, channels = (samples.shape[1], samples.shape[2], samples.shape[3])
    moments = jnp.arange(micro_count + sections - 1, dtype=jnp.int32)
    blank = jnp.zeros((frames, pixels, channels), jnp.bfloat16)

    sp_rows = spatial_weight.shape[1]
    tm_rows = temporal_weight.shape[1]
    own_rows = jnp.concatenate([spatial_weight[0], temporal_weight[0]], axis=0)
    gathered = lax.all_gather(own_rows, "dp", axis=0, tiled=False)
    full_spatial = gathered[:, :sp_rows].reshape(n_dp * sp_rows, channels)
    full_temporal = gathered[:, sp_rows:].reshape(n_dp * tm_rows, channels)

    embeddings = jax.vmap(lambda s: embedding_of(s, channels))(timesteps)

    def slot_of(position):
        return jnp.clip(position, -1, micro_count) + 1

    def stash_put(stash, value, slot):
        return lax.dynamic_update_index_in_dim(stash, value, slot, 0)

    def forward_step(carry, moment):
        incoming, s_in, s_normed, s_preact, s_act = carry
        position = moment - section_index
        picked = jnp.clip(position, 0, micro_count - 1)
        slot = slot_of(position)
        own = lax.dynamic_index_in_dim(samples, picked, 0, keepdims=False)
        embedding = lax.dynamic_index_in_dim(embeddings, picked, 0, keepdims=False)
        block_in = jnp.where(section_index == 0, own, incoming)
        result, normed, preact, activated = section_forward(
            block_in, embedding, full_spatial, full_temporal
        )
        s_in = stash_put(s_in, block_in, slot)
        s_normed = stash_put(s_normed, normed.reshape(frames, pixels, channels), slot)
        s_preact = stash_put(s_preact, preact, slot)
        s_act = stash_put(s_act, activated, slot)
        passed = passed_along(result, "pipe", 1)
        return ((passed, s_in, s_normed, s_preact, s_act), None)

    slots = micro_count + 2
    start = (
        blank,
        jnp.zeros((slots, frames, pixels, channels), jnp.bfloat16),
        jnp.zeros((slots, frames, pixels, channels), jnp.bfloat16),
        jnp.zeros((slots, frames, pixels, channels), jnp.float32),
        jnp.zeros((slots, frames, pixels, channels), jnp.bfloat16),
    )
    (_, s_in, s_normed, s_preact, s_act), _ = lax.scan(forward_step, start, moments)

    def backward_step(carry, moment):
        incoming, s_pre, s_up = carry
        position = moment - (sections - 1 - section_index)
        picked = jnp.clip(position, 0, micro_count - 1)
        slot = slot_of(position)
        stored = jnp.clip(position, 0, micro_count - 1) + 1
        block_in = lax.dynamic_index_in_dim(s_in, stored, 0, keepdims=False)
        preact = lax.dynamic_index_in_dim(s_preact, stored, 0, keepdims=False)
        embedding = lax.dynamic_index_in_dim(embeddings, picked, 0, keepdims=False)
        given = lax.dynamic_index_in_dim(cotangent, picked, 0, keepdims=False)
        upstream = jnp.where(section_index == sections - 1, given, incoming)
        back_input, pre_grad = section_backward(
            block_in, embedding, full_spatial, full_temporal, upstream, preact
        )
        s_pre = stash_put(s_pre, pre_grad, slot)
        s_up = stash_put(s_up, upstream, slot)
        passed = passed_along(back_input, "pipe", -1)
        return ((passed, s_pre, s_up), None)

    start = (
        blank,
        jnp.zeros((slots, frames, pixels, channels), jnp.bfloat16),
        jnp.zeros((slots, frames, pixels, channels), jnp.bfloat16),
    )
    (_, s_pre, s_up), _ = lax.scan(backward_step, start, moments)

    normed_all = s_normed[1 : micro_count + 1]
    act_all = s_act[1 : micro_count + 1]
    pre_all = s_pre[1 : micro_count + 1].reshape(-1, channels)
    up_all = s_up[1 : micro_count + 1].reshape(-1, channels)
    spatial_term = lax.dot_general(
        spatial_columns(normed_all), pre_all, (((0,), (0,)), ((), ())),
        preferred_element_type=jnp.float32,
    )
    temporal_term = lax.dot_general(
        temporal_columns(act_all), up_all, (((0,), (0,)), ((), ())),
        preferred_element_type=jnp.float32,
    )
    partial_rows = jnp.concatenate(
        [
            spatial_term.astype(jnp.bfloat16).reshape(n_dp, sp_rows, channels),
            temporal_term.astype(jnp.bfloat16).reshape(n_dp, tm_rows, channels),
        ],
        axis=1,
    )
    share = lax.psum_scatter(partial_rows, "dp", scatter_dimension=0, tiled=False)
    share = share.astype(jnp.float32)
    return (share[None, :sp_rows], share[None, sp_rows:])


def solution(mesh):
    return jax.shard_map(
        per_device,
        mesh=mesh,
        in_specs=(
            P("dp", None, None, None),
            P("dp"),
            P("dp", None, None, None),
            P("pipe", "dp", None),
            P("pipe", "dp", None),
        ),
        out_specs=(P("pipe", "dp", None), P("pipe", "dp", None)),
        check_vma=False,
    )
```

```python
import functools
import math

import jax
import jax.numpy as jnp
from jax import lax
from jax.experimental import pallas as pl
from jax.experimental.pallas import tpu as pltpu
from jax.sharding import PartitionSpec as P

HEIGHT = 8
WIDTH = 4


def hop_kernel(steps, x_ref, out_ref, landing, send_sem, recv_sem):
    count = lax.axis_size("pipe")
    me = lax.axis_index("pipe")
    row = lax.axis_index("dp")
    dest = me + steps
    src = me - steps
    has_dest = (dest >= 0) & (dest < count)
    has_src = (src >= 0) & (src < count)
    barrier = pltpu.get_barrier_semaphore()
    copy = pltpu.make_async_remote_copy(
        src_ref=x_ref,
        dst_ref=landing,
        send_sem=send_sem,
        recv_sem=recv_sem,
        device_id=(dest, row),
        device_id_type=pl.DeviceIdType.MESH,
    )

    @pl.when(has_src)
    def _():
        pl.semaphore_signal(barrier, inc=1, device_id=(src, row), device_id_type=pl.DeviceIdType.MESH)

    @pl.when(has_dest)
    def _():
        pl.semaphore_wait(barrier, 1)
        copy.start()

    @pl.when(has_src)
    def _():
        copy.wait_recv()
        out_ref[...] = landing[...]

    @pl.when(jnp.logical_not(has_src))
    def _():
        out_ref[...] = jnp.zeros_like(out_ref)

    @pl.when(has_dest)
    def _():
        copy.wait_send()


def passed_along(value, axis, steps):
    assert axis == "pipe"
    return pl.pallas_call(
        functools.partial(hop_kernel, steps),
        out_shape=jax.ShapeDtypeStruct(value.shape, value.dtype),
        in_specs=[pl.BlockSpec(memory_space=pltpu.VMEM)],
        out_specs=pl.BlockSpec(memory_space=pltpu.VMEM),
        scratch_shapes=[
            pltpu.VMEM(value.shape, value.dtype),
            pltpu.SemaphoreType.DMA(()),
            pltpu.SemaphoreType.DMA(()),
        ],
        compiler_params=pltpu.CompilerParams(
            collective_id=0 if steps > 0 else 1, has_side_effects=True
        ),
    )(value)


def embedding_of(step, channels):
    half_width = channels // 2
    frequency = jnp.exp(-math.log(10000.0) * jnp.arange(half_width, dtype=jnp.float32) / half_width)
    phases = step.astype(jnp.float32) * frequency
    return jnp.concatenate([jnp.sin(phases), jnp.cos(phases)])


def normalize(summed):
    return summed * lax.rsqrt(jnp.mean(summed * summed, axis=-1, keepdims=True) + 1e-06)


def spatial_columns(normed):
    lead = normed.shape[:-2]
    channels = normed.shape[-1]
    grid = normed.reshape(lead + (HEIGHT, WIDTH, channels))
    pad = [(0, 0)] * len(lead) + [(1, 1), (1, 1), (0, 0)]
    padded = jnp.pad(grid, pad)
    pieces = [
        padded[..., row : row + HEIGHT, col : col + WIDTH, :] for row in range(3) for col in range(3)
    ]
    return jnp.concatenate(pieces, axis=-1).reshape(-1, 9 * channels)


def spatial_fold(grads, frames, channels):
    parts = grads.reshape(frames, HEIGHT, WIDTH, 9, channels)
    total = None
    for row in range(3):
        for col in range(3):
            piece = jnp.pad(
                parts[:, :, :, row * 3 + col, :],
                ((0, 0), (row, 2 - row), (col, 2 - col), (0, 0)),
            )
            total = piece if total is None else total + piece
    return total[:, 1 : HEIGHT + 1, 1 : WIDTH + 1, :].reshape(frames, HEIGHT * WIDTH, channels)


def temporal_columns(activated):
    lead = activated.shape[:-3]
    frames = activated.shape[-3]
    channels = activated.shape[-1]
    pad = [(0, 0)] * len(lead) + [(1, 1), (0, 0), (0, 0)]
    padded = jnp.pad(activated, pad)
    pieces = [padded[..., tap : tap + frames, :, :] for tap in range(3)]
    return jnp.concatenate(pieces, axis=-1).reshape(-1, 3 * channels)


def temporal_fold(grads, frames, pixels, channels):
    parts = grads.reshape(frames, pixels, 3, channels)
    total = None
    for tap in range(3):
        piece = jnp.pad(parts[:, :, tap, :], ((tap, 2 - tap), (0, 0), (0, 0)))
        total = piece if total is None else total + piece
    return total[1 : frames + 1]


def section_forward(block_in, embedding, spatial, temporal):
    frames, pixels, channels = block_in.shape
    summed = block_in.astype(jnp.float32) + embedding
    normed = normalize(summed).astype(jnp.bfloat16)
    preact = jnp.dot(spatial_columns(normed), spatial, preferred_element_type=jnp.float32)
    activated = jax.nn.silu(preact).astype(jnp.bfloat16).reshape(frames, pixels, channels)
    mixed = jnp.dot(temporal_columns(activated), temporal, preferred_element_type=jnp.float32)
    out = (block_in.astype(jnp.float32) + mixed.reshape(frames, pixels, channels)).astype(
        jnp.bfloat16
    )
    return out, normed, preact.reshape(frames, pixels, channels), activated


def section_backward(block_in, embedding, spatial, temporal, upstream, preact):
    frames, pixels, channels = block_in.shape
    summed = block_in.astype(jnp.float32) + embedding
    upstream_flat = upstream.reshape(frames * pixels, channels)
    act_grad = temporal_fold(
        jnp.dot(upstream_flat, temporal.T, preferred_element_type=jnp.float32),
        frames,
        pixels,
        channels,
    )
    logistic = jax.nn.sigmoid(preact)
    slope = logistic * (1.0 + preact * (1.0 - logistic))
    pre_grad = (act_grad * slope).astype(jnp.bfloat16)
    norm_grad = spatial_fold(
        jnp.dot(
            pre_grad.reshape(frames * pixels, channels),
            spatial.T,
            preferred_element_type=jnp.float32,
        ),
        frames,
        channels,
    )
    _, pullback = jax.vjp(normalize, summed)
    back_input = (upstream.astype(jnp.float32) + pullback(norm_grad)[0]).astype(jnp.bfloat16)
    return back_input, pre_grad


def scatter_kernel(part_hbm, out_ref, landing, send_sem, recv_sem, own_sem):
    count = lax.axis_size("dp")
    me = lax.axis_index("dp")
    stage = lax.axis_index("pipe")
    barrier = pltpu.get_barrier_semaphore()

    own = pltpu.make_async_copy(part_hbm.at[me], landing.at[me], own_sem)
    own.start()

    def greet(peer, carry):
        @pl.when(peer != me)
        def _():
            pl.semaphore_signal(
                barrier, inc=1, device_id=(stage, peer), device_id_type=pl.DeviceIdType.MESH
            )
        return carry

    lax.fori_loop(0, count, greet, 0)
    pl.semaphore_wait(barrier, count - 1)

    def remote(peer):
        return pltpu.make_async_remote_copy(
            src_ref=part_hbm.at[peer],
            dst_ref=landing.at[me],
            send_sem=send_sem.at[peer],
            recv_sem=recv_sem.at[me],
            device_id=(stage, peer),
            device_id_type=pl.DeviceIdType.MESH,
        )

    def send(step, carry):
        peer = lax.rem(me + step, count)
        remote(peer).start()
        return carry

    lax.fori_loop(1, count, send, 0)
    own.wait()

    def take(step, total):
        peer = lax.rem(me + count - step, count)
        pltpu.make_async_remote_copy(
            src_ref=part_hbm.at[peer],
            dst_ref=landing.at[peer],
            send_sem=send_sem.at[peer],
            recv_sem=recv_sem.at[peer],
            device_id=(stage, peer),
            device_id_type=pl.DeviceIdType.MESH,
        ).wait_recv()
        return total + landing[peer].astype(jnp.float32)

    total = lax.fori_loop(1, count, take, landing[me].astype(jnp.float32))
    out_ref[...] = total

    def drain(step, carry):
        peer = lax.rem(me + step, count)
        remote(peer).wait_send()
        return carry

    lax.fori_loop(1, count, drain, 0)


def scatter_sum(partial_rows):
    count, rows, channels = partial_rows.shape
    return pl.pallas_call(
        scatter_kernel,
        out_shape=jax.ShapeDtypeStruct((rows, channels), jnp.float32),
        in_specs=[pl.BlockSpec(memory_space=pl.ANY)],
        out_specs=pl.BlockSpec(memory_space=pltpu.VMEM),
        scratch_shapes=[
            pltpu.VMEM((count, rows, channels), partial_rows.dtype),
            pltpu.SemaphoreType.DMA((count,)),
            pltpu.SemaphoreType.DMA((count,)),
            pltpu.SemaphoreType.DMA(()),
        ],
        compiler_params=pltpu.CompilerParams(
            collective_id=2, has_side_effects=True, vmem_limit_bytes=48 * 1024 * 1024
        ),
    )(partial_rows)


def per_device(samples, timesteps, cotangent, spatial_weight, temporal_weight):
    sections = lax.axis_size("pipe")
    n_dp = lax.axis_size("dp")
    section_index = lax.axis_index("pipe")
    micro_count = samples.shape[0]
    frames, pixels, channels = (samples.shape[1], samples.shape[2], samples.shape[3])
    moments = jnp.arange(micro_count + sections - 1, dtype=jnp.int32)
    blank = jnp.zeros((frames, pixels, channels), jnp.bfloat16)

    sp_rows = spatial_weight.shape[1]
    tm_rows = temporal_weight.shape[1]
    own_rows = jnp.concatenate([spatial_weight[0], temporal_weight[0]], axis=0)
    gathered = lax.all_gather(own_rows, "dp", axis=0, tiled=False)
    full_spatial = gathered[:, :sp_rows].reshape(n_dp * sp_rows, channels)
    full_temporal = gathered[:, sp_rows:].reshape(n_dp * tm_rows, channels)

    embeddings = jax.vmap(lambda s: embedding_of(s, channels))(timesteps)

    def slot_of(position):
        return jnp.clip(position, -1, micro_count) + 1

    def stash_put(stash, value, slot):
        return lax.dynamic_update_index_in_dim(stash, value, slot, 0)

    def forward_step(carry, moment):
        incoming, s_in, s_normed, s_preact, s_act = carry
        position = moment - section_index
        picked = jnp.clip(position, 0, micro_count - 1)
        slot = slot_of(position)
        own = lax.dynamic_index_in_dim(samples, picked, 0, keepdims=False)
        embedding = lax.dynamic_index_in_dim(embeddings, picked, 0, keepdims=False)
        block_in = jnp.where(section_index == 0, own, incoming)
        result, normed, preact, activated = section_forward(
            block_in, embedding, full_spatial, full_temporal
        )
        s_in = stash_put(s_in, block_in, slot)
        s_normed = stash_put(s_normed, normed.reshape(frames, pixels, channels), slot)
        s_preact = stash_put(s_preact, preact, slot)
        s_act = stash_put(s_act, activated, slot)
        passed = passed_along(result, "pipe", 1)
        return ((passed, s_in, s_normed, s_preact, s_act), None)

    slots = micro_count + 2
    start = (
        blank,
        jnp.zeros((slots, frames, pixels, channels), jnp.bfloat16),
        jnp.zeros((slots, frames, pixels, channels), jnp.bfloat16),
        jnp.zeros((slots, frames, pixels, channels), jnp.float32),
        jnp.zeros((slots, frames, pixels, channels), jnp.bfloat16),
    )
    (_, s_in, s_normed, s_preact, s_act), _ = lax.scan(forward_step, start, moments)

    def backward_step(carry, moment):
        incoming, s_pre, s_up = carry
        position = moment - (sections - 1 - section_index)
        picked = jnp.clip(position, 0, micro_count - 1)
        slot = slot_of(position)
        stored = jnp.clip(position, 0, micro_count - 1) + 1
        block_in = lax.dynamic_index_in_dim(s_in, stored, 0, keepdims=False)
        preact = lax.dynamic_index_in_dim(s_preact, stored, 0, keepdims=False)
        embedding = lax.dynamic_index_in_dim(embeddings, picked, 0, keepdims=False)
        given = lax.dynamic_index_in_dim(cotangent, picked, 0, keepdims=False)
        upstream = jnp.where(section_index == sections - 1, given, incoming)
        back_input, pre_grad = section_backward(
            block_in, embedding, full_spatial, full_temporal, upstream, preact
        )
        s_pre = stash_put(s_pre, pre_grad, slot)
        s_up = stash_put(s_up, upstream, slot)
        passed = passed_along(back_input, "pipe", -1)
        return ((passed, s_pre, s_up), None)

    start = (
        blank,
        jnp.zeros((slots, frames, pixels, channels), jnp.bfloat16),
        jnp.zeros((slots, frames, pixels, channels), jnp.bfloat16),
    )
    (_, s_pre, s_up), _ = lax.scan(backward_step, start, moments)

    normed_all = s_normed[1 : micro_count + 1]
    act_all = s_act[1 : micro_count + 1]
    pre_all = s_pre[1 : micro_count + 1].reshape(-1, channels)
    up_all = s_up[1 : micro_count + 1].reshape(-1, channels)
    spatial_term = lax.dot_general(
        spatial_columns(normed_all), pre_all, (((0,), (0,)), ((), ())),
        preferred_element_type=jnp.float32,
    )
    temporal_term = lax.dot_general(
        temporal_columns(act_all), up_all, (((0,), (0,)), ((), ())),
        preferred_element_type=jnp.float32,
    )
    partial_rows = jnp.concatenate(
        [
            spatial_term.astype(jnp.bfloat16).reshape(n_dp, sp_rows, channels),
            temporal_term.astype(jnp.bfloat16).reshape(n_dp, tm_rows, channels),
        ],
        axis=1,
    )
    share = scatter_sum(partial_rows)
    return (share[None, :sp_rows], share[None, sp_rows:])


def solution(mesh):
    return jax.shard_map(
        per_device,
        mesh=mesh,
        in_specs=(
            P("dp", None, None, None),
            P("dp"),
            P("dp", None, None, None),
            P("pipe", "dp", None),
            P("pipe", "dp", None),
        ),
        out_specs=(P("pipe", "dp", None), P("pipe", "dp", None)),
        check_vma=False,
    )
```

```python
import functools
import math

import jax
import jax.numpy as jnp
from jax import lax
from jax.experimental import pallas as pl
from jax.experimental.pallas import tpu as pltpu
from jax.sharding import PartitionSpec as P

HEIGHT = 8
WIDTH = 4


def hop_kernel(steps, x_ref, out_ref, landing, send_sem, recv_sem):
    count = lax.axis_size("pipe")
    me = lax.axis_index("pipe")
    row = lax.axis_index("dp")
    dest = me + steps
    src = me - steps
    has_dest = (dest >= 0) & (dest < count)
    has_src = (src >= 0) & (src < count)
    barrier = pltpu.get_barrier_semaphore()
    copy = pltpu.make_async_remote_copy(
        src_ref=x_ref,
        dst_ref=landing,
        send_sem=send_sem,
        recv_sem=recv_sem,
        device_id=(dest, row),
        device_id_type=pl.DeviceIdType.MESH,
    )

    @pl.when(has_src)
    def _():
        pl.semaphore_signal(barrier, inc=1, device_id=(src, row), device_id_type=pl.DeviceIdType.MESH)

    @pl.when(has_dest)
    def _():
        pl.semaphore_wait(barrier, 1)
        copy.start()

    @pl.when(has_src)
    def _():
        copy.wait_recv()
        out_ref[...] = landing[...]

    @pl.when(jnp.logical_not(has_src))
    def _():
        out_ref[...] = jnp.zeros_like(out_ref)

    @pl.when(has_dest)
    def _():
        copy.wait_send()


def passed_along(value, axis, steps):
    assert axis == "pipe"
    return pl.pallas_call(
        functools.partial(hop_kernel, steps),
        out_shape=jax.ShapeDtypeStruct(value.shape, value.dtype),
        in_specs=[pl.BlockSpec(memory_space=pltpu.VMEM)],
        out_specs=pl.BlockSpec(memory_space=pltpu.VMEM),
        scratch_shapes=[
            pltpu.VMEM(value.shape, value.dtype),
            pltpu.SemaphoreType.DMA(()),
            pltpu.SemaphoreType.DMA(()),
        ],
        compiler_params=pltpu.CompilerParams(
            collective_id=0 if steps > 0 else 1, has_side_effects=True
        ),
    )(value)


def embedding_of(step, channels):
    half_width = channels // 2
    frequency = jnp.exp(-math.log(10000.0) * jnp.arange(half_width, dtype=jnp.float32) / half_width)
    phases = step.astype(jnp.float32) * frequency
    return jnp.concatenate([jnp.sin(phases), jnp.cos(phases)])


def normalize(summed):
    return summed * lax.rsqrt(jnp.mean(summed * summed, axis=-1, keepdims=True) + 1e-06)


def spatial_columns(normed):
    lead = normed.shape[:-2]
    channels = normed.shape[-1]
    grid = normed.reshape(lead + (HEIGHT, WIDTH, channels))
    pad = [(0, 0)] * len(lead) + [(1, 1), (1, 1), (0, 0)]
    padded = jnp.pad(grid, pad)
    pieces = [
        padded[..., row : row + HEIGHT, col : col + WIDTH, :] for row in range(3) for col in range(3)
    ]
    return jnp.concatenate(pieces, axis=-1).reshape(-1, 9 * channels)


def spatial_fold(grads, frames, channels):
    parts = grads.reshape(frames, HEIGHT, WIDTH, 9, channels)
    total = None
    for row in range(3):
        for col in range(3):
            piece = jnp.pad(
                parts[:, :, :, row * 3 + col, :],
                ((0, 0), (row, 2 - row), (col, 2 - col), (0, 0)),
            )
            total = piece if total is None else total + piece
    return total[:, 1 : HEIGHT + 1, 1 : WIDTH + 1, :].reshape(frames, HEIGHT * WIDTH, channels)


def temporal_columns(activated):
    lead = activated.shape[:-3]
    frames = activated.shape[-3]
    channels = activated.shape[-1]
    pad = [(0, 0)] * len(lead) + [(1, 1), (0, 0), (0, 0)]
    padded = jnp.pad(activated, pad)
    pieces = [padded[..., tap : tap + frames, :, :] for tap in range(3)]
    return jnp.concatenate(pieces, axis=-1).reshape(-1, 3 * channels)


def temporal_fold(grads, frames, pixels, channels):
    parts = grads.reshape(frames, pixels, 3, channels)
    total = None
    for tap in range(3):
        piece = jnp.pad(parts[:, :, tap, :], ((tap, 2 - tap), (0, 0), (0, 0)))
        total = piece if total is None else total + piece
    return total[1 : frames + 1]


def section_forward(block_in, embedding, spatial, temporal):
    frames, pixels, channels = block_in.shape
    summed = block_in.astype(jnp.float32) + embedding
    normed = normalize(summed).astype(jnp.bfloat16)
    preact = jnp.dot(spatial_columns(normed), spatial, preferred_element_type=jnp.float32)
    activated = jax.nn.silu(preact).astype(jnp.bfloat16).reshape(frames, pixels, channels)
    mixed = jnp.dot(temporal_columns(activated), temporal, preferred_element_type=jnp.float32)
    out = (block_in.astype(jnp.float32) + mixed.reshape(frames, pixels, channels)).astype(
        jnp.bfloat16
    )
    return out, normed, preact.reshape(frames, pixels, channels), activated


def section_backward(block_in, embedding, spatial, temporal, upstream, preact):
    frames, pixels, channels = block_in.shape
    summed = block_in.astype(jnp.float32) + embedding
    upstream_flat = upstream.reshape(frames * pixels, channels)
    act_grad = temporal_fold(
        jnp.dot(upstream_flat, temporal.T, preferred_element_type=jnp.float32),
        frames,
        pixels,
        channels,
    )
    logistic = jax.nn.sigmoid(preact)
    slope = logistic * (1.0 + preact * (1.0 - logistic))
    pre_grad = (act_grad * slope).astype(jnp.bfloat16)
    norm_grad = spatial_fold(
        jnp.dot(
            pre_grad.reshape(frames * pixels, channels),
            spatial.T,
            preferred_element_type=jnp.float32,
        ),
        frames,
        channels,
    )
    _, pullback = jax.vjp(normalize, summed)
    back_input = (upstream.astype(jnp.float32) + pullback(norm_grad)[0]).astype(jnp.bfloat16)
    return back_input, pre_grad


def per_device(samples, timesteps, cotangent, spatial_weight, temporal_weight):
    sections = lax.axis_size("pipe")
    n_dp = lax.axis_size("dp")
    section_index = lax.axis_index("pipe")
    micro_count = samples.shape[0]
    frames, pixels, channels = (samples.shape[1], samples.shape[2], samples.shape[3])
    moments = jnp.arange(micro_count + sections - 1, dtype=jnp.int32)
    blank = jnp.zeros((frames, pixels, channels), jnp.bfloat16)

    sp_rows = spatial_weight.shape[1]
    tm_rows = temporal_weight.shape[1]
    own_rows = jnp.concatenate([spatial_weight[0], temporal_weight[0]], axis=0)
    gathered = lax.all_gather(own_rows, "dp", axis=0, tiled=False)
    full_spatial = gathered[:, :sp_rows].reshape(n_dp * sp_rows, channels)
    full_temporal = gathered[:, sp_rows:].reshape(n_dp * tm_rows, channels)

    embeddings = jax.vmap(lambda s: embedding_of(s, channels))(timesteps)

    def slot_of(position):
        return jnp.clip(position, -1, micro_count) + 1

    def stash_put(stash, value, slot):
        return lax.dynamic_update_index_in_dim(stash, value, slot, 0)

    def forward_step(carry, moment):
        incoming, s_in, s_normed, s_preact, s_act = carry
        position = moment - section_index
        picked = jnp.clip(position, 0, micro_count - 1)
        slot = slot_of(position)
        own = lax.dynamic_index_in_dim(samples, picked, 0, keepdims=False)
        embedding = lax.dynamic_index_in_dim(embeddings, picked, 0, keepdims=False)
        block_in = jnp.where(section_index == 0, own, incoming)
        result, normed, preact, activated = section_forward(
            block_in, embedding, full_spatial, full_temporal
        )
        s_in = stash_put(s_in, block_in, slot)
        s_normed = stash_put(s_normed, normed.reshape(frames, pixels, channels), slot)
        s_preact = stash_put(s_preact, preact, slot)
        s_act = stash_put(s_act, activated, slot)
        passed = passed_along(result, "pipe", 1)
        return ((passed, s_in, s_normed, s_preact, s_act), None)

    slots = micro_count + 2
    start = (
        blank,
        jnp.zeros((slots, frames, pixels, channels), jnp.bfloat16),
        jnp.zeros((slots, frames, pixels, channels), jnp.bfloat16),
        jnp.zeros((slots, frames, pixels, channels), jnp.float32),
        jnp.zeros((slots, frames, pixels, channels), jnp.bfloat16),
    )
    (_, s_in, s_normed, s_preact, s_act), _ = lax.scan(forward_step, start, moments)

    def backward_step(carry, moment):
        incoming, s_pre, s_up = carry
        position = moment - (sections - 1 - section_index)
        picked = jnp.clip(position, 0, micro_count - 1)
        slot = slot_of(position)
        stored = jnp.clip(position, 0, micro_count - 1) + 1
        block_in = lax.dynamic_index_in_dim(s_in, stored, 0, keepdims=False)
        preact = lax.dynamic_index_in_dim(s_preact, stored, 0, keepdims=False)
        embedding = lax.dynamic_index_in_dim(embeddings, picked, 0, keepdims=False)
        given = lax.dynamic_index_in_dim(cotangent, picked, 0, keepdims=False)
        upstream = jnp.where(section_index == sections - 1, given, incoming)
        back_input, pre_grad = section_backward(
            block_in, embedding, full_spatial, full_temporal, upstream, preact
        )
        s_pre = stash_put(s_pre, pre_grad, slot)
        s_up = stash_put(s_up, upstream, slot)
        passed = passed_along(back_input, "pipe", -1)
        return ((passed, s_pre, s_up), None)

    start = (
        blank,
        jnp.zeros((slots, frames, pixels, channels), jnp.bfloat16),
        jnp.zeros((slots, frames, pixels, channels), jnp.bfloat16),
    )
    (_, s_pre, s_up), _ = lax.scan(backward_step, start, moments)

    normed_all = s_normed[1 : micro_count + 1]
    act_all = s_act[1 : micro_count + 1]
    pre_all = s_pre[1 : micro_count + 1].reshape(-1, channels)
    up_all = s_up[1 : micro_count + 1].reshape(-1, channels)
    grid_all = jnp.pad(
        normed_all.reshape(micro_count, frames, HEIGHT, WIDTH, channels),
        ((0, 0), (0, 0), (1, 1), (1, 1), (0, 0)),
    )
    spatial_term = jnp.concatenate(
        [
            lax.dot_general(
                grid_all[:, :, row : row + HEIGHT, col : col + WIDTH, :].reshape(-1, channels),
                pre_all,
                (((0,), (0,)), ((), ())),
                preferred_element_type=jnp.float32,
            )
            for row in range(3)
            for col in range(3)
        ],
        axis=0,
    )
    temporal_term = lax.dot_general(
        temporal_columns(act_all), up_all, (((0,), (0,)), ((), ())),
        preferred_element_type=jnp.float32,
    )
    partial_rows = jnp.concatenate(
        [
            spatial_term.astype(jnp.bfloat16).reshape(n_dp, sp_rows, channels),
            temporal_term.astype(jnp.bfloat16).reshape(n_dp, tm_rows, channels),
        ],
        axis=1,
    )
    share = lax.psum_scatter(partial_rows, "dp", scatter_dimension=0, tiled=False)
    share = share.astype(jnp.float32)
    return (share[None, :sp_rows], share[None, sp_rows:])


def solution(mesh):
    return jax.shard_map(
        per_device,
        mesh=mesh,
        in_specs=(
            P("dp", None, None, None),
            P("dp"),
            P("dp", None, None, None),
            P("pipe", "dp", None),
            P("pipe", "dp", None),
        ),
        out_specs=(P("pipe", "dp", None), P("pipe", "dp", None)),
        check_vma=False,
    )
```

```python
import math

import jax
import jax.numpy as jnp
from jax import lax
from jax.sharding import PartitionSpec as P

HEIGHT = 8
WIDTH = 4


def passed_along(value, axis, steps):
    count = lax.axis_size(axis)
    first, last = (max(0, -steps), min(count, count - steps))
    return lax.ppermute(value, axis, [(source, source + steps) for source in range(first, last)])


def embedding_of(step, channels):
    half_width = channels // 2
    frequency = jnp.exp(-math.log(10000.0) * jnp.arange(half_width, dtype=jnp.float32) / half_width)
    phases = step.astype(jnp.float32) * frequency
    return jnp.concatenate([jnp.sin(phases), jnp.cos(phases)])


def normalize(summed):
    return summed * lax.rsqrt(jnp.mean(summed * summed, axis=-1, keepdims=True) + 1e-06)


def spatial_columns(normed):
    lead = normed.shape[:-2]
    channels = normed.shape[-1]
    grid = normed.reshape(lead + (HEIGHT, WIDTH, channels))
    pad = [(0, 0)] * len(lead) + [(1, 1), (1, 1), (0, 0)]
    padded = jnp.pad(grid, pad)
    pieces = [
        padded[..., row : row + HEIGHT, col : col + WIDTH, :] for row in range(3) for col in range(3)
    ]
    return jnp.concatenate(pieces, axis=-1).reshape(-1, 9 * channels)


def spatial_fold(grads, frames, channels):
    parts = grads.reshape(frames, HEIGHT, WIDTH, 9, channels)
    total = None
    for row in range(3):
        for col in range(3):
            piece = jnp.pad(
                parts[:, :, :, row * 3 + col, :],
                ((0, 0), (row, 2 - row), (col, 2 - col), (0, 0)),
            )
            total = piece if total is None else total + piece
    return total[:, 1 : HEIGHT + 1, 1 : WIDTH + 1, :].reshape(frames, HEIGHT * WIDTH, channels)


def temporal_columns(activated):
    lead = activated.shape[:-3]
    frames = activated.shape[-3]
    channels = activated.shape[-1]
    pad = [(0, 0)] * len(lead) + [(1, 1), (0, 0), (0, 0)]
    padded = jnp.pad(activated, pad)
    pieces = [padded[..., tap : tap + frames, :, :] for tap in range(3)]
    return jnp.concatenate(pieces, axis=-1).reshape(-1, 3 * channels)


def temporal_fold(grads, frames, pixels, channels):
    parts = grads.reshape(frames, pixels, 3, channels)
    total = None
    for tap in range(3):
        piece = jnp.pad(parts[:, :, tap, :], ((tap, 2 - tap), (0, 0), (0, 0)))
        total = piece if total is None else total + piece
    return total[1 : frames + 1]


def section_forward(block_in, embedding, spatial, temporal):
    frames, pixels, channels = block_in.shape
    summed = block_in.astype(jnp.float32) + embedding
    normed = normalize(summed).astype(jnp.bfloat16)
    preact = jnp.dot(spatial_columns(normed), spatial, preferred_element_type=jnp.float32)
    activated = jax.nn.silu(preact).astype(jnp.bfloat16).reshape(frames, pixels, channels)
    mixed = jnp.dot(temporal_columns(activated), temporal, preferred_element_type=jnp.float32)
    out = (block_in.astype(jnp.float32) + mixed.reshape(frames, pixels, channels)).astype(
        jnp.bfloat16
    )
    return out, normed, preact.reshape(frames, pixels, channels), activated


def section_backward(block_in, embedding, spatial, temporal, upstream, preact):
    frames, pixels, channels = block_in.shape
    summed = block_in.astype(jnp.float32) + embedding
    upstream_flat = upstream.reshape(frames * pixels, channels)
    act_grad = temporal_fold(
        jnp.dot(upstream_flat, temporal.T, preferred_element_type=jnp.float32),
        frames,
        pixels,
        channels,
    )
    logistic = jax.nn.sigmoid(preact)
    slope = logistic * (1.0 + preact * (1.0 - logistic))
    pre_grad = (act_grad * slope).astype(jnp.bfloat16)
    norm_grad = spatial_fold(
        jnp.dot(
            pre_grad.reshape(frames * pixels, channels),
            spatial.T,
            preferred_element_type=jnp.float32,
        ),
        frames,
        channels,
    )
    _, pullback = jax.vjp(normalize, summed)
    back_input = (upstream.astype(jnp.float32) + pullback(norm_grad)[0]).astype(jnp.bfloat16)
    return back_input, pre_grad


def per_device(samples, timesteps, cotangent, spatial_weight, temporal_weight):
    sections = lax.axis_size("pipe")
    n_dp = lax.axis_size("dp")
    section_index = lax.axis_index("pipe")
    micro_count = samples.shape[0]
    frames, pixels, channels = (samples.shape[1], samples.shape[2], samples.shape[3])
    moments = jnp.arange(micro_count + sections - 1, dtype=jnp.int32)
    blank = jnp.zeros((frames, pixels, channels), jnp.bfloat16)

    sp_rows = spatial_weight.shape[1]
    tm_rows = temporal_weight.shape[1]
    own_rows = jnp.concatenate([spatial_weight[0], temporal_weight[0]], axis=0)
    gathered = lax.all_gather(own_rows, "dp", axis=0, tiled=False)
    full_spatial = gathered[:, :sp_rows].reshape(n_dp * sp_rows, channels)
    full_temporal = gathered[:, sp_rows:].reshape(n_dp * tm_rows, channels)

    embeddings = jax.vmap(lambda s: embedding_of(s, channels))(timesteps)

    def slot_of(position):
        return jnp.clip(position, -1, micro_count) + 1

    def stash_put(stash, value, slot):
        return lax.dynamic_update_index_in_dim(stash, value, slot, 0)

    def forward_step(incoming, moment):
        position = moment - section_index
        picked = jnp.clip(position, 0, micro_count - 1)
        own = lax.dynamic_index_in_dim(samples, picked, 0, keepdims=False)
        embedding = lax.dynamic_index_in_dim(embeddings, picked, 0, keepdims=False)
        block_in = jnp.where(section_index == 0, own, incoming)
        result, normed, preact, activated = section_forward(
            block_in, embedding, full_spatial, full_temporal
        )
        passed = passed_along(result, "pipe", 1)
        return passed, (block_in, normed.reshape(frames, pixels, channels), preact, activated)

    _, (s_in, s_normed, s_preact, s_act) = lax.scan(forward_step, blank, moments)

    def backward_step(incoming, moment):
        position = moment - (sections - 1 - section_index)
        picked = jnp.clip(position, 0, micro_count - 1)
        stored = picked + section_index
        block_in = lax.dynamic_index_in_dim(s_in, stored, 0, keepdims=False)
        preact = lax.dynamic_index_in_dim(s_preact, stored, 0, keepdims=False)
        embedding = lax.dynamic_index_in_dim(embeddings, picked, 0, keepdims=False)
        given = lax.dynamic_index_in_dim(cotangent, picked, 0, keepdims=False)
        upstream = jnp.where(section_index == sections - 1, given, incoming)
        back_input, pre_grad = section_backward(
            block_in, embedding, full_spatial, full_temporal, upstream, preact
        )
        passed = passed_along(back_input, "pipe", -1)
        return passed, (pre_grad, upstream)

    _, (s_pre, s_up) = lax.scan(backward_step, blank, moments)

    normed_all = lax.dynamic_slice_in_dim(s_normed, section_index, micro_count, 0)
    act_all = lax.dynamic_slice_in_dim(s_act, section_index, micro_count, 0)
    back_first = sections - 1 - section_index
    pre_all = lax.dynamic_slice_in_dim(s_pre, back_first, micro_count, 0).reshape(-1, channels)
    up_all = lax.dynamic_slice_in_dim(s_up, back_first, micro_count, 0).reshape(-1, channels)
    spatial_term = lax.dot_general(
        spatial_columns(normed_all), pre_all, (((0,), (0,)), ((), ())),
        preferred_element_type=jnp.float32,
    )
    temporal_term = lax.dot_general(
        temporal_columns(act_all), up_all, (((0,), (0,)), ((), ())),
        preferred_element_type=jnp.float32,
    )
    partial_rows = jnp.concatenate(
        [
            spatial_term.astype(jnp.bfloat16).reshape(n_dp, sp_rows, channels),
            temporal_term.astype(jnp.bfloat16).reshape(n_dp, tm_rows, channels),
        ],
        axis=1,
    )
    share = lax.psum_scatter(partial_rows, "dp", scatter_dimension=0, tiled=False)
    share = share.astype(jnp.float32)
    return (share[None, :sp_rows], share[None, sp_rows:])


def solution(mesh):
    return jax.shard_map(
        per_device,
        mesh=mesh,
        in_specs=(
            P("dp", None, None, None),
            P("dp"),
            P("dp", None, None, None),
            P("pipe", "dp", None),
            P("pipe", "dp", None),
        ),
        out_specs=(P("pipe", "dp", None), P("pipe", "dp", None)),
        check_vma=False,
    )
```

```python
import math

import jax
import jax.numpy as jnp
from jax import lax
from jax.sharding import PartitionSpec as P

HEIGHT = 8
WIDTH = 4


def passed_along(value, axis, steps):
    count = lax.axis_size(axis)
    first, last = (max(0, -steps), min(count, count - steps))
    return lax.ppermute(value, axis, [(source, source + steps) for source in range(first, last)])


def embedding_of(step, channels):
    half_width = channels // 2
    frequency = jnp.exp(-math.log(10000.0) * jnp.arange(half_width, dtype=jnp.float32) / half_width)
    phases = step.astype(jnp.float32) * frequency
    return jnp.concatenate([jnp.sin(phases), jnp.cos(phases)])


def normalize(summed):
    return summed * lax.rsqrt(jnp.mean(summed * summed, axis=-1, keepdims=True) + 1e-06)


def spatial_columns(normed):
    lead = normed.shape[:-2]
    channels = normed.shape[-1]
    grid = normed.reshape(lead + (HEIGHT, WIDTH, channels))
    pad = [(0, 0)] * len(lead) + [(1, 1), (1, 1), (0, 0)]
    padded = jnp.pad(grid, pad)
    pieces = [
        padded[..., row : row + HEIGHT, col : col + WIDTH, :] for row in range(3) for col in range(3)
    ]
    return jnp.concatenate(pieces, axis=-1).reshape(-1, 9 * channels)


def spatial_fold(grads, frames, channels):
    parts = grads.reshape(frames, HEIGHT, WIDTH, 9, channels)
    total = None
    for row in range(3):
        for col in range(3):
            piece = jnp.pad(
                parts[:, :, :, row * 3 + col, :],
                ((0, 0), (row, 2 - row), (col, 2 - col), (0, 0)),
            )
            total = piece if total is None else total + piece
    return total[:, 1 : HEIGHT + 1, 1 : WIDTH + 1, :].reshape(frames, HEIGHT * WIDTH, channels)


def temporal_columns(activated):
    lead = activated.shape[:-3]
    frames = activated.shape[-3]
    channels = activated.shape[-1]
    pad = [(0, 0)] * len(lead) + [(1, 1), (0, 0), (0, 0)]
    padded = jnp.pad(activated, pad)
    pieces = [padded[..., tap : tap + frames, :, :] for tap in range(3)]
    return jnp.concatenate(pieces, axis=-1).reshape(-1, 3 * channels)


def temporal_fold(grads, frames, pixels, channels):
    parts = grads.reshape(frames, pixels, 3, channels)
    total = None
    for tap in range(3):
        piece = jnp.pad(parts[:, :, tap, :], ((tap, 2 - tap), (0, 0), (0, 0)))
        total = piece if total is None else total + piece
    return total[1 : frames + 1]


def section_forward(block_in, embedding, spatial, temporal):
    frames, pixels, channels = block_in.shape
    summed = block_in.astype(jnp.float32) + embedding
    normed = normalize(summed).astype(jnp.bfloat16)
    preact = jnp.dot(spatial_columns(normed), spatial, preferred_element_type=jnp.float32)
    activated = jax.nn.silu(preact).astype(jnp.bfloat16).reshape(frames, pixels, channels)
    mixed = jnp.dot(temporal_columns(activated), temporal, preferred_element_type=jnp.float32)
    out = (block_in.astype(jnp.float32) + mixed.reshape(frames, pixels, channels)).astype(
        jnp.bfloat16
    )
    return out, normed, preact.reshape(frames, pixels, channels), activated


def section_backward(block_in, embedding, spatial, temporal, upstream, preact):
    frames, pixels, channels = block_in.shape
    summed = block_in.astype(jnp.float32) + embedding
    upstream_flat = upstream.reshape(frames * pixels, channels)
    act_grad = temporal_fold(
        jnp.dot(upstream_flat, temporal.T, preferred_element_type=jnp.float32),
        frames,
        pixels,
        channels,
    )
    logistic = jax.nn.sigmoid(preact)
    slope = logistic * (1.0 + preact * (1.0 - logistic))
    pre_grad = (act_grad * slope).astype(jnp.bfloat16)
    norm_grad = spatial_fold(
        jnp.dot(
            pre_grad.reshape(frames * pixels, channels),
            spatial.T,
            preferred_element_type=jnp.float32,
        ),
        frames,
        channels,
    )
    _, pullback = jax.vjp(normalize, summed)
    back_input = (upstream.astype(jnp.float32) + pullback(norm_grad)[0]).astype(jnp.bfloat16)
    return back_input, pre_grad


def per_device(samples, timesteps, cotangent, spatial_weight, temporal_weight):
    sections = lax.axis_size("pipe")
    n_dp = lax.axis_size("dp")
    section_index = lax.axis_index("pipe")
    micro_count = samples.shape[0]
    frames, pixels, channels = (samples.shape[1], samples.shape[2], samples.shape[3])
    moments = jnp.arange(micro_count + sections - 1, dtype=jnp.int32)
    blank = jnp.zeros((frames, pixels, channels), jnp.bfloat16)

    sp_rows = spatial_weight.shape[1]
    tm_rows = temporal_weight.shape[1]
    own_rows = jnp.concatenate([spatial_weight[0], temporal_weight[0]], axis=0)
    gathered = lax.all_gather(own_rows, "dp", axis=0, tiled=False)
    full_spatial = gathered[:, :sp_rows].reshape(n_dp * sp_rows, channels)
    full_temporal = gathered[:, sp_rows:].reshape(n_dp * tm_rows, channels)

    embeddings = jax.vmap(lambda s: embedding_of(s, channels))(timesteps)

    def slot_of(position):
        return jnp.clip(position, -1, micro_count) + 1

    def stash_put(stash, value, slot):
        return lax.dynamic_update_index_in_dim(stash, value, slot, 0)

    def forward_step(carry, moment):
        incoming, s_in, s_normed, s_preact, s_act = carry
        position = moment - section_index
        picked = jnp.clip(position, 0, micro_count - 1)
        slot = slot_of(position)
        own = lax.dynamic_index_in_dim(samples, picked, 0, keepdims=False)
        embedding = lax.dynamic_index_in_dim(embeddings, picked, 0, keepdims=False)
        block_in = jnp.where(section_index == 0, own, incoming)
        result, normed, preact, activated = section_forward(
            block_in, embedding, full_spatial, full_temporal
        )
        s_in = stash_put(s_in, block_in, slot)
        s_normed = stash_put(s_normed, normed.reshape(frames, pixels, channels), slot)
        s_preact = stash_put(s_preact, preact, slot)
        s_act = stash_put(s_act, activated, slot)
        passed = passed_along(result, "pipe", 1)
        return ((passed, s_in, s_normed, s_preact, s_act), None)

    slots = micro_count + 2
    start = (
        blank,
        jnp.zeros((slots, frames, pixels, channels), jnp.bfloat16),
        jnp.zeros((slots, frames, pixels, channels), jnp.bfloat16),
        jnp.zeros((slots, frames, pixels, channels), jnp.float32),
        jnp.zeros((slots, frames, pixels, channels), jnp.bfloat16),
    )
    (_, s_in, s_normed, s_preact, s_act), _ = lax.scan(forward_step, start, moments)

    def backward_step(carry, moment):
        incoming, s_pre, s_up = carry
        position = moment - (sections - 1 - section_index)
        picked = jnp.clip(position, 0, micro_count - 1)
        slot = slot_of(position)
        stored = jnp.clip(position, 0, micro_count - 1) + 1
        block_in = lax.dynamic_index_in_dim(s_in, stored, 0, keepdims=False)
        preact = lax.dynamic_index_in_dim(s_preact, stored, 0, keepdims=False)
        embedding = lax.dynamic_index_in_dim(embeddings, picked, 0, keepdims=False)
        given = lax.dynamic_index_in_dim(cotangent, picked, 0, keepdims=False)
        upstream = jnp.where(section_index == sections - 1, given, incoming)
        back_input, pre_grad = section_backward(
            block_in, embedding, full_spatial, full_temporal, upstream, preact
        )
        s_pre = stash_put(s_pre, pre_grad, slot)
        s_up = stash_put(s_up, upstream, slot)
        passed = passed_along(back_input, "pipe", -1)
        return ((passed, s_pre, s_up), None)

    start = (
        blank,
        jnp.zeros((slots, frames, pixels, channels), jnp.bfloat16),
        jnp.zeros((slots, frames, pixels, channels), jnp.bfloat16),
    )
    (_, s_pre, s_up), _ = lax.scan(backward_step, start, moments)

    normed_all = s_normed[1 : micro_count + 1]
    act_all = s_act[1 : micro_count + 1]
    pre_all = s_pre[1 : micro_count + 1].reshape(-1, channels)
    up_all = s_up[1 : micro_count + 1].reshape(-1, channels)
    spatial_term = lax.dot_general(
        spatial_columns(normed_all).reshape(-1, n_dp, sp_rows), pre_all, (((0,), (0,)), ((), ())),
        preferred_element_type=jnp.float32,
    )
    temporal_term = lax.dot_general(
        temporal_columns(act_all).reshape(-1, n_dp, tm_rows), up_all, (((0,), (0,)), ((), ())),
        preferred_element_type=jnp.float32,
    )
    partial_rows = jnp.concatenate(
        [spatial_term.astype(jnp.bfloat16), temporal_term.astype(jnp.bfloat16)],
        axis=1,
    )
    share = lax.psum_scatter(partial_rows, "dp", scatter_dimension=0, tiled=False)
    share = share.astype(jnp.float32)
    return (share[None, :sp_rows], share[None, sp_rows:])


def solution(mesh):
    return jax.shard_map(
        per_device,
        mesh=mesh,
        in_specs=(
            P("dp", None, None, None),
            P("dp"),
            P("dp", None, None, None),
            P("pipe", "dp", None),
            P("pipe", "dp", None),
        ),
        out_specs=(P("pipe", "dp", None), P("pipe", "dp", None)),
        check_vma=False,
    )
```

```python
import math

import jax
import jax.numpy as jnp
from jax import lax
from jax.sharding import PartitionSpec as P

HEIGHT = 8
WIDTH = 4


def passed_along(value, axis, steps):
    count = lax.axis_size(axis)
    first, last = (max(0, -steps), min(count, count - steps))
    return lax.ppermute(value, axis, [(source, source + steps) for source in range(first, last)])


def embedding_of(step, channels):
    half_width = channels // 2
    frequency = jnp.exp(-math.log(10000.0) * jnp.arange(half_width, dtype=jnp.float32) / half_width)
    phases = step.astype(jnp.float32) * frequency
    return jnp.concatenate([jnp.sin(phases), jnp.cos(phases)])


def normalize(summed):
    return summed * lax.rsqrt(jnp.mean(summed * summed, axis=-1, keepdims=True) + 1e-06)


def spatial_columns(normed):
    lead = normed.shape[:-2]
    channels = normed.shape[-1]
    grid = normed.reshape(lead + (HEIGHT, WIDTH, channels))
    pad = [(0, 0)] * len(lead) + [(1, 1), (1, 1), (0, 0)]
    padded = jnp.pad(grid, pad)
    pieces = [
        padded[..., row : row + HEIGHT, col : col + WIDTH, :] for row in range(3) for col in range(3)
    ]
    return jnp.concatenate(pieces, axis=-1).reshape(-1, 9 * channels)


def spatial_fold(grads, frames, channels):
    parts = grads.reshape(frames, HEIGHT, WIDTH, 9, channels)
    total = None
    for row in range(3):
        for col in range(3):
            piece = jnp.pad(
                parts[:, :, :, row * 3 + col, :],
                ((0, 0), (row, 2 - row), (col, 2 - col), (0, 0)),
            )
            total = piece if total is None else total + piece
    return total[:, 1 : HEIGHT + 1, 1 : WIDTH + 1, :].reshape(frames, HEIGHT * WIDTH, channels)


def temporal_columns(activated):
    lead = activated.shape[:-3]
    frames = activated.shape[-3]
    channels = activated.shape[-1]
    pad = [(0, 0)] * len(lead) + [(1, 1), (0, 0), (0, 0)]
    padded = jnp.pad(activated, pad)
    pieces = [padded[..., tap : tap + frames, :, :] for tap in range(3)]
    return jnp.concatenate(pieces, axis=-1).reshape(-1, 3 * channels)


def temporal_fold(grads, frames, pixels, channels):
    parts = grads.reshape(frames, pixels, 3, channels)
    total = None
    for tap in range(3):
        piece = jnp.pad(parts[:, :, tap, :], ((tap, 2 - tap), (0, 0), (0, 0)))
        total = piece if total is None else total + piece
    return total[1 : frames + 1]


def section_forward(block_in, embedding, spatial, temporal):
    frames, pixels, channels = block_in.shape
    summed = block_in.astype(jnp.float32) + embedding
    normed = normalize(summed).astype(jnp.bfloat16)
    preact = jnp.dot(spatial_columns(normed), spatial, preferred_element_type=jnp.float32)
    activated = jax.nn.silu(preact).astype(jnp.bfloat16).reshape(frames, pixels, channels)
    mixed = jnp.dot(temporal_columns(activated), temporal, preferred_element_type=jnp.float32)
    out = (block_in.astype(jnp.float32) + mixed.reshape(frames, pixels, channels)).astype(
        jnp.bfloat16
    )
    return out, normed, preact.reshape(frames, pixels, channels), activated


def section_backward(block_in, embedding, spatial, temporal, upstream, preact):
    frames, pixels, channels = block_in.shape
    summed = block_in.astype(jnp.float32) + embedding
    upstream_flat = upstream.reshape(frames * pixels, channels)
    act_grad = temporal_fold(
        jnp.dot(upstream_flat, temporal.T, preferred_element_type=jnp.float32),
        frames,
        pixels,
        channels,
    )
    logistic = jax.nn.sigmoid(preact)
    slope = logistic * (1.0 + preact * (1.0 - logistic))
    pre_grad = (act_grad * slope).astype(jnp.bfloat16)
    norm_grad = spatial_fold(
        jnp.dot(
            pre_grad.reshape(frames * pixels, channels),
            spatial.T,
            preferred_element_type=jnp.float32,
        ),
        frames,
        channels,
    )
    _, pullback = jax.vjp(normalize, summed)
    back_input = (upstream.astype(jnp.float32) + pullback(norm_grad)[0]).astype(jnp.bfloat16)
    return back_input, pre_grad


def per_device(samples, timesteps, cotangent, spatial_weight, temporal_weight):
    sections = lax.axis_size("pipe")
    n_dp = lax.axis_size("dp")
    section_index = lax.axis_index("pipe")
    micro_count = samples.shape[0]
    frames, pixels, channels = (samples.shape[1], samples.shape[2], samples.shape[3])
    moments = jnp.arange(micro_count + sections - 1, dtype=jnp.int32)
    blank = jnp.zeros((frames, pixels, channels), jnp.bfloat16)

    sp_rows = spatial_weight.shape[1]
    tm_rows = temporal_weight.shape[1]
    own_rows = jnp.concatenate([spatial_weight[0], temporal_weight[0]], axis=0)
    gathered = lax.all_gather(own_rows, "dp", axis=0, tiled=False)
    full_spatial = gathered[:, :sp_rows].reshape(n_dp * sp_rows, channels)
    full_temporal = gathered[:, sp_rows:].reshape(n_dp * tm_rows, channels)

    embeddings = jax.vmap(lambda s: embedding_of(s, channels))(timesteps)

    def slot_of(position):
        return jnp.clip(position, -1, micro_count) + 1

    def stash_put(stash, value, slot):
        return lax.dynamic_update_index_in_dim(stash, value, slot, 0)

    def forward_step(carry, moment):
        incoming, s_in, s_normed, s_preact, s_act = carry
        position = moment - section_index
        picked = jnp.clip(position, 0, micro_count - 1)
        slot = slot_of(position)
        own = lax.dynamic_index_in_dim(samples, picked, 0, keepdims=False)
        embedding = lax.dynamic_index_in_dim(embeddings, picked, 0, keepdims=False)
        block_in = jnp.where(section_index == 0, own, incoming)
        result, normed, preact, activated = section_forward(
            block_in, embedding, full_spatial, full_temporal
        )
        s_in = stash_put(s_in, block_in, slot)
        s_normed = stash_put(s_normed, normed.reshape(frames, pixels, channels), slot)
        s_preact = stash_put(s_preact, preact, slot)
        s_act = stash_put(s_act, activated, slot)
        passed = passed_along(result, "pipe", 1)
        return ((passed, s_in, s_normed, s_preact, s_act), None)

    slots = micro_count + 2
    start = (
        blank,
        jnp.zeros((slots, frames, pixels, channels), jnp.bfloat16),
        jnp.zeros((slots, frames, pixels, channels), jnp.bfloat16),
        jnp.zeros((slots, frames, pixels, channels), jnp.float32),
        jnp.zeros((slots, frames, pixels, channels), jnp.bfloat16),
    )
    (_, s_in, s_normed, s_preact, s_act), _ = lax.scan(forward_step, start, moments, unroll=2)

    def backward_step(carry, moment):
        incoming, s_pre, s_up = carry
        position = moment - (sections - 1 - section_index)
        picked = jnp.clip(position, 0, micro_count - 1)
        slot = slot_of(position)
        stored = jnp.clip(position, 0, micro_count - 1) + 1
        block_in = lax.dynamic_index_in_dim(s_in, stored, 0, keepdims=False)
        preact = lax.dynamic_index_in_dim(s_preact, stored, 0, keepdims=False)
        embedding = lax.dynamic_index_in_dim(embeddings, picked, 0, keepdims=False)
        given = lax.dynamic_index_in_dim(cotangent, picked, 0, keepdims=False)
        upstream = jnp.where(section_index == sections - 1, given, incoming)
        back_input, pre_grad = section_backward(
            block_in, embedding, full_spatial, full_temporal, upstream, preact
        )
        s_pre = stash_put(s_pre, pre_grad, slot)
        s_up = stash_put(s_up, upstream, slot)
        passed = passed_along(back_input, "pipe", -1)
        return ((passed, s_pre, s_up), None)

    start = (
        blank,
        jnp.zeros((slots, frames, pixels, channels), jnp.bfloat16),
        jnp.zeros((slots, frames, pixels, channels), jnp.bfloat16),
    )
    (_, s_pre, s_up), _ = lax.scan(backward_step, start, moments, unroll=2)

    normed_all = s_normed[1 : micro_count + 1]
    act_all = s_act[1 : micro_count + 1]
    pre_all = s_pre[1 : micro_count + 1].reshape(-1, channels)
    up_all = s_up[1 : micro_count + 1].reshape(-1, channels)
    spatial_term = lax.dot_general(
        spatial_columns(normed_all), pre_all, (((0,), (0,)), ((), ())),
        preferred_element_type=jnp.float32,
    )
    temporal_term = lax.dot_general(
        temporal_columns(act_all), up_all, (((0,), (0,)), ((), ())),
        preferred_element_type=jnp.float32,
    )
    partial_rows = jnp.concatenate(
        [
            spatial_term.astype(jnp.bfloat16).reshape(n_dp, sp_rows, channels),
            temporal_term.astype(jnp.bfloat16).reshape(n_dp, tm_rows, channels),
        ],
        axis=1,
    )
    share = lax.psum_scatter(partial_rows, "dp", scatter_dimension=0, tiled=False)
    share = share.astype(jnp.float32)
    return (share[None, :sp_rows], share[None, sp_rows:])


def solution(mesh):
    return jax.shard_map(
        per_device,
        mesh=mesh,
        in_specs=(
            P("dp", None, None, None),
            P("dp"),
            P("dp", None, None, None),
            P("pipe", "dp", None),
            P("pipe", "dp", None),
        ),
        out_specs=(P("pipe", "dp", None), P("pipe", "dp", None)),
        check_vma=False,
    )
```
